128 devices in a mesh: gx: 8 (over x, core), gy: 16 (over z, y).
Axes of the slice: x: 4, y: 4, z: 4, core: 2. Of those that a mesh axis runs over, the one named last changes fastest.
Arguments:
- multipole: bfloat16 [65536, 256], P(('gx', 'gy')), may hold values from -6 to 6
- coarse_local: bfloat16 [256, 256], P('gx'), may hold values from -6 to 6
- send_rows: int32 [128, 128, 16], P(('gx', 'gy')), may hold values from 0 to 511
- list_src: int32 [65536, 64], P(('gx', 'gy')), may hold values from 0 to 2559
- list_vec: int32 [65536, 64], P(('gx', 'gy')), may hold values from 0 to 15
- list_len: int32 [65536], P(('gx', 'gy')), may hold values from 16 to 64, as said below
- parent_of: int32 [65536], P(('gx', 'gy')), may hold values from 0 to 255
- octant: int32 [65536], P(('gx', 'gy')), may hold values from 0 to 7
- m2l_ops: bfloat16 [16, 256, 256], replicated, may hold values from -0.0625 to 0.0625
- l2l_ops: bfloat16 [8, 256, 256], replicated, may hold values from -0.375 to 0.375
- near_list: int32 [65536, 8], P(('gx', 'gy')), may hold values from 0 to 575, as said below
- positions: float32 [3, 2097152], P(None, ('gx', 'gy')), may hold values from 0 to 1
- charges: float32 [2097152], P(('gx', 'gy')), may hold values from -0.75 to 0.75
- basis: bfloat16 [2097152, 256], P(('gx', 'gy')), may hold values from -0.375 to 0.375
Outputs:
- leaf_local: float32 [65536, 256], P(('gx', 'gy'))
- potential: float32 [2097152], P(('gx', 'gy'))
The draws below stay inside these ranges and needn't reach their ends.
Inputs may be any that keep to these rules, and one draw needn't show every extreme that they name: `list_len`: the first cell of every device uses all 64 slots. `near_list`: cell i of a device lists extended cells i to i + 64.
All inputs are finite; a program needn't handle non-finite values.
Results may differ from the reference program's by a relative error of at most 0.0024.
Values may be sent and summed in bfloat16 or wider, within the bound.
A program may use at most 64 MiB of HBM per device.

```python
import jax
import jax.numpy as jnp
from jax import lax

P_SIZE = 256
CELLS_DEV = 512
PART = 32
LIST = 64
NVEC = 16
SLOTS = 16
NEAR = 8
RIM = 32
CELLS = 65536
PARTICLES = 2097152
TABLE = 2560
COARSE = 256
N_GX = 8
N_GY = 16
DEVICES = 128


def draw_list_len(key, part):
    values = jax.random.randint(key, (CELLS,), LIST // 4, LIST + 1)
    first = jnp.arange(CELLS) % CELLS_DEV == 0
    return jnp.where(first, LIST, values).astype(jnp.int32)


def draw_near_list(key, part):
    offsets = jax.random.randint(key, (CELLS, NEAR), -RIM, RIM + 1)
    place = jnp.arange(CELLS) % CELLS_DEV
    column = jnp.arange(NEAR)[None, :] == 0
    offsets = jnp.where(column & (place[:, None] == 0), -RIM, offsets)
    offsets = jnp.where(column & (place[:, None] == CELLS_DEV - 1), RIM, offsets)
    return (place[:, None] + RIM + offsets).astype(jnp.int32)


def plant(drawn, own_key, low, largest):
    shape = drawn.shape
    spot = [jax.random.randint(jax.random.fold_in(own_key, axis), (), 0, shape[axis]) for axis in range(len(shape))]
    drawn = drawn.at[tuple(spot)].set(low)
    longest = shape.index(max(shape))
    spot[longest] = (spot[longest] + 1) % shape[longest]
    return drawn.at[tuple(spot)].set(largest)


def steps_of(rng, shape, cuts, smallest, top_value):
    level, own = 1.0, jax.random.fold_in(rng, 6)
    for position, parts in cuts:
        draws = jnp.exp(jax.random.uniform(jax.random.fold_in(own, position), (parts,), jnp.float32, smallest / len(cuts), top_value / len(cuts)))
        level = level * jnp.repeat(draws, shape[position] // parts).reshape([-1 if axis == position else 1 for axis in range(len(shape))])
    return level


def noise(rng, extent, spread, reach, cuts=(), kind=jnp.bfloat16):
    gain = steps_of(rng, extent, cuts, -0.22, 0.18) if cuts else 1.0
    result = jax.random.normal(rng, extent, jnp.float32) * spread * gain
    return jnp.minimum(jnp.maximum(result, -reach), reach).astype(kind)


def setup_inputs(seed: int = 0) -> dict:
    splits = jax.random.split(jax.random.key(seed), 15)
    return {
        "multipole": noise(splits[0], (CELLS, P_SIZE), 1.0, 6.0, ((0, 128),)),
        "coarse_local": noise(splits[1], (COARSE, P_SIZE), 1.0, 6.0, ((0, 8),)),
        "send_rows": plant(jax.random.randint(splits[2], (DEVICES, DEVICES, SLOTS), 0, CELLS_DEV), jax.random.fold_in(splits[2], 1), 0, CELLS_DEV - 1).astype(jnp.int32),
        "list_src": plant(jax.random.randint(splits[3], (CELLS, LIST), 0, TABLE), jax.random.fold_in(splits[3], 1), 0, TABLE - 1).astype(jnp.int32),
        "list_vec": plant(jax.random.randint(splits[4], (CELLS, LIST), 0, NVEC), jax.random.fold_in(splits[4], 1), 0, NVEC - 1).astype(jnp.int32),
        "list_len": draw_list_len(jax.random.fold_in(splits[14], 71), 0),
        "parent_of": plant(jax.random.randint(splits[6], (CELLS,), 0, COARSE), jax.random.fold_in(splits[6], 1), 0, COARSE - 1).astype(jnp.int32),
        "octant": plant(jax.random.randint(splits[7], (CELLS,), 0, 8), jax.random.fold_in(splits[7], 1), 0, 7).astype(jnp.int32),
        "m2l_ops": noise(splits[8], (NVEC, P_SIZE, P_SIZE), (P_SIZE * LIST // 2) ** -0.5, 0.0625),
        "l2l_ops": noise(splits[9], (8, P_SIZE, P_SIZE), P_SIZE ** -0.5, 0.375),
        "near_list": draw_near_list(jax.random.fold_in(splits[14], 71), 0),
        "positions": jnp.clip(1.0 * jax.random.uniform(splits[11], (3, PARTICLES), jnp.float32) ** steps_of(splits[11], (3, PARTICLES), ((1, 128),), -0.2, 0.2), 0.0, 1.0),
        "charges": noise(splits[12], (PARTICLES,), 0.05, 0.75, ((0, 128),), jnp.float32),
        "basis": noise(splits[13], (PARTICLES, P_SIZE), P_SIZE ** -0.5, 0.375, ((0, 128),)),
    }


softening = 0.01

def translate_far(table, src, vec, lengths, m2l_ops):
    rows = table[src].astype(jnp.float32)
    classes = jnp.arange(NVEC, dtype=jnp.int32)
    slot_iota = jnp.arange(LIST, dtype=jnp.int32)
    select = ((vec[:, :, None] == classes[None, None, :]) & (slot_iota[None, :, None] < lengths[:, None, None])).astype(jnp.float32)
    grouped = jnp.einsum('ckv,ckp->cvp', select, rows).astype(jnp.bfloat16)
    return jnp.einsum('cvp,vpq->cq', grouped.astype(jnp.float32), m2l_ops.astype(jnp.float32))

def near_sum(targets, tiles):
    total = jnp.zeros((targets.shape[1], targets.shape[2], tiles.shape[2]), jnp.float32)
    for axis_index in range(3):
        gap = targets[axis_index][:, :, None] - tiles[axis_index][:, None, :]
        total = total + gap * gap
    return lax.optimization_barrier(jnp.sum(tiles[3][:, None, :] * lax.rsqrt(total + softening), axis=2))

def reference(multipole, coarse_local, send_rows, list_src, list_vec, list_len, parent_of, octant, m2l_ops, l2l_ops, near_list, positions, charges, basis):
    ndevices = N_GX * N_GY
    offsets = jnp.arange(ndevices, dtype=jnp.int32) * CELLS_DEV

    def far_device(device):
        start = (device * CELLS_DEV).astype(jnp.int32)
        own = lax.dynamic_slice_in_dim(multipole, start, CELLS_DEV, 0)
        rows = (send_rows[:, device, :] + offsets[:, None]).reshape(-1)
        table = jnp.concatenate([own, multipole[rows]], axis=0)
        src = lax.dynamic_slice_in_dim(list_src, start, CELLS_DEV, 0)
        vec = lax.dynamic_slice_in_dim(list_vec, start, CELLS_DEV, 0)
        lengths = lax.dynamic_slice_in_dim(list_len, start, CELLS_DEV, 0)
        return translate_far(table, src, vec, lengths, m2l_ops)
    far = lax.map(far_device, jnp.arange(ndevices, dtype=jnp.int32)).reshape(CELLS, P_SIZE)
    shifted = jnp.einsum('cp,opq->coq', coarse_local.astype(jnp.float32), l2l_ops.astype(jnp.float32))
    down = shifted.reshape(COARSE * 8, P_SIZE)[parent_of * 8 + octant]
    leaf_local = far + down
    rounded = leaf_local.astype(jnp.bfloat16).astype(jnp.float32)
    farpot = jnp.einsum('cjp,cp->cj', basis.reshape(CELLS, PART, P_SIZE).astype(jnp.float32), rounded).reshape(PARTICLES)
    data = jnp.concatenate([positions, charges[None, :]], axis=0)
    padded = jnp.pad(data, ((0, 0), (RIM * PART, RIM * PART)))

    def near_device(device):
        start = (device * CELLS_DEV).astype(jnp.int32)
        extended = lax.dynamic_slice_in_dim(padded, start * PART, (CELLS_DEV + 2 * RIM) * PART, 1)
        extended = extended.reshape(4, CELLS_DEV + 2 * RIM, PART)
        neighbors = lax.dynamic_slice_in_dim(near_list, start, CELLS_DEV, 0)
        tiles = extended[:, neighbors].reshape(4, CELLS_DEV, NEAR * PART)
        targets = lax.dynamic_slice_in_dim(positions, start * PART, CELLS_DEV * PART, 1).reshape(3, CELLS_DEV, PART)
        return near_sum(targets, tiles)
    nearpot = lax.map(near_device, jnp.arange(ndevices, dtype=jnp.int32)).reshape(PARTICLES)
    return (leaf_local, farpot + nearpot)
```

```python
import functools

import jax
import jax.numpy as jnp
from jax import lax
from jax.experimental import pallas as pl
from jax.experimental.pallas import tpu as pltpu
from jax.sharding import PartitionSpec as P

BF = jnp.bfloat16
F8 = jnp.float8_e4m3fn
F32 = jnp.float32
I32 = jnp.int32
SOFT = 0.01


def iota(shape, axis):
    return lax.broadcasted_iota(I32, shape, axis)


def dot(a, b):
    return jnp.dot(a, b, preferred_element_type=F32)


def dot_nt(a, b):
    return lax.dot_general(a, b, (((1,), (1,)), ((), ())), preferred_element_type=F32)


def column(row):
    return jnp.broadcast_to(row, (128, 128)).T


def lanes(x, idx):
    return jnp.take_along_axis(x, idx, axis=1, mode="promise_in_bounds")


def onehot(rows, code):
    ids = iota((rows, 128), 0).astype(F32).astype(BF)
    return jnp.where(ids == jnp.broadcast_to(code, (rows, 128)).astype(BF), jnp.ones((), BF), jnp.zeros((), BF)).astype(F8)


def codes(src_ref, vec_ref, len_ref, hi0, hi1, lo):
    parts = []
    for b in range(4):
        rows = pl.ds(128 * b, 128)
        used = iota((128, 64), 1) < column(len_ref[pl.ds(b, 1), :].astype(F32))[:, :64].astype(I32)
        src = src_ref[rows, :]
        high = jnp.where(used, vec_ref[rows, :] + 16 * (src >> 8), -1).astype(F32)
        parts.append((high, (src & 255).astype(F32)))
    for b in range(2):
        rows = pl.ds(128 * b, 128)
        high = jnp.concatenate([parts[b][0], parts[b + 2][0]], 1)
        first = iota((128, 128), 1) < 64
        hi0[rows, :] = jnp.where(first, high, -1.0)
        hi1[rows, :] = jnp.where(first, -1.0, high)
        lo[rows, :] = jnp.concatenate([parts[b][1], parts[b + 2][1]], 1)


def count_pair(p, hi0, hi1, lo, S):
    a = jnp.concatenate([onehot(160, hi0[pl.ds(p, 1), :]), onehot(160, hi1[pl.ds(p, 1), :])], 0)
    s = dot_nt(a, onehot(256, lo[pl.ds(p, 1), :])).astype(BF)
    for t in range(10):
        S[t, p] = s[16 * t : 16 * t + 16]
        S[t, p + 256] = s[160 + 16 * t : 176 + 16 * t]


def near_prepare(E, near_ref, XT, Y, tgt, src):
    for f in range(4):
        for h in range(2):
            XT[f, h] = E[f, pl.ds(128 * h, 128), :].T
        own = E[f, pl.ds(8, 128), :].T if f < 3 else None
        lane = iota((32, 128), 1)
        for b in range(5):
            y = None
            for q in range(4):
                g = lanes(XT[f, b // 4, pl.ds(32 * q, 32), :], 32 * (b % 4) + (lane >> 2))
                y = g if q == 0 else jnp.where((lane & 3) == q, g, y)
            Y[f, b] = y
        if f < 3:
            for b in range(4):
                y = None
                for q in range(4):
                    g = lanes(own[32 * q : 32 * q + 32], 32 * b + (lane >> 2))
                    y = g if q == 0 else jnp.where((lane & 3) == q, g, y)
                tgt[b, f] = y
    for b in range(4):
        listed = near_ref[pl.ds(128 * b, 128), :].astype(F32)
        listed = jnp.concatenate([listed, jnp.zeros((128, 120), F32)], 1).T
        for n in range(8):
            idx = jnp.broadcast_to(listed[n : n + 1].astype(I32) - 128 * b, (32, 128))
            inside, wrapped = idx < 128, idx & 127
            for f in range(4):
                g = jnp.where(inside, lanes(Y[f, b], wrapped), lanes(Y[f, b + 1], wrapped))
                for s in range(4):
                    src[b, 4 * n + s, f] = g[8 * s : 8 * s + 8]


def near_unit(b, jj, J, tgt, src, N):
    ts = [
        [jnp.broadcast_to(tgt[b, f, pl.ds(jj * J + j, 1), :], (8, 128)) for f in range(3)] for j in range(J)
    ]
    acc = [jnp.zeros((8, 128), F32) for _ in range(J)]
    for m in range(32):
        x, y, z, q = (src[b, m, f] for f in range(4))
        for j in range(J):
            dx, dy, dz = x - ts[j][0], y - ts[j][1], z - ts[j][2]
            acc[j] = acc[j] + q * lax.rsqrt(dx * dx + dy * dy + (dz * dz + SOFT))
    for j in range(J):
        N[b, pl.ds(jj * J + j, 1), :] = jnp.sum(acc[j], 0, keepdims=True)


def near_rows(N):
    lane = iota((32, 128), 1)
    parts = []
    for q in range(4):
        z = None
        for b in range(4):
            g = lanes(N[b], 4 * (lane & 31) + q)
            z = g if b == 0 else jnp.where((lane >> 5) == b, g, z)
        parts.append(z)
    return jnp.concatenate(parts, 0).T


def group(i, n, table, S, G, Gb):
    rows = 16 * n
    lhs = jnp.concatenate([S[t, pl.ds(i * n, n)].reshape(rows, 256) for t in range(10)], 1)
    g = dot(lhs, table[...])
    G[0] = g[:, :128]
    G[1] = g[:, 128:]
    for v in range(16):
        Gb[v, pl.ds(i * n, n), :] = jnp.concatenate(
            [G[0, pl.ds(v, n, stride=16), :], G[1, pl.ds(v, n, stride=16), :]], 1
        ).astype(BF)


def coarse_rows(parent_ref, octant_ref, coarse, Gb):
    for b in range(4):
        parent = column(parent_ref[pl.ds(b, 1), :].astype(F32))
        octant = column(octant_ref[pl.ds(b, 1), :].astype(F32))
        lane = iota((128, 128), 1).astype(F32)
        pick = jnp.concatenate([(parent == lane).astype(F32), (parent == lane + 128.0).astype(F32)], 1).astype(BF)
        rows = dot(pick, coarse[...])
        octant = jnp.concatenate([octant, octant], 1)
        for o in range(8):
            Gb[16 + o, pl.ds(128 * b, 128), :] = jnp.where(octant == float(o), rows, 0.0).astype(BF)


def far_rows(i, S, rounded, F):
    pieces = []
    for c in range(16):
        pieces += [S[0, i * 16 + c], S[1, i * 16 + c]]
    r = dot_nt(rounded[pl.ds(pl.multiple_of(16 * i, 16), 16), :], jnp.concatenate(pieces, 0))
    r = jnp.where(iota((16, 512), 0) == (iota((16, 512), 1) >> 5), r, 0.0)
    r = jnp.sum(r, 0, keepdims=True)
    for h in range(4):
        F[pl.ds(4 * i + h, 1), :] = r[:, 128 * h : 128 * h + 128]


NBLK = 64


def kernel(
    table_ref, coarse_ref, src_ref, vec_ref, len_ref, parent_ref, octant_ref, near_ref, ext_ref, m2l_hbm, l2l_hbm, basis_hbm,
    leaf_ref, pot_ref,
    S, G, Gb, ops, rounded, hi0, hi1, lo, XT, Y, tgt, src, N, F, sem_ops, sem_basis,
):
    ops_in = [
        pltpu.make_async_copy(m2l_hbm, ops.at[pl.ds(0, 16)], sem_ops.at[0]),
        pltpu.make_async_copy(l2l_hbm, ops.at[pl.ds(16, 8)], sem_ops.at[1]),
    ]
    for c in ops_in:
        c.start()
    codes(src_ref, vec_ref, len_ref, hi0, hi1, lo)
    lax.fori_loop(0, 256, lambda p, _: count_pair(p, hi0, hi1, lo, S), None, unroll=32)
    near_prepare(ext_ref, near_ref, XT, Y, tgt, src)
    for b in range(4):
        lax.fori_loop(0, 8, lambda jj, _: near_unit(b, jj, 4, tgt, src, N), None)
    coarse_rows(parent_ref, octant_ref, coarse_ref, Gb)

    def basis_copy(i, h):
        cells = pl.ds(i * NBLK, NBLK)
        return pltpu.make_async_copy(basis_hbm.at[cells, h], S.at[h, cells], sem_basis.at[i, h])

    def block(i, _):
        group(i, NBLK, table_ref, S, G, Gb)
        basis_copy(i, 0).start()
        basis_copy(i, 1).start()

    lax.fori_loop(0, 512 // NBLK, block, None)
    for c in ops_in:
        c.wait()
    for h in range(2):
        rows = pl.ds(256 * h, 256)
        leaf = dot(
            jnp.concatenate([Gb[v, rows, :] for v in range(24)], 1), ops[...].reshape(24 * 256, 256)
        )
        leaf_ref[rows, :] = leaf
        rounded[rows, :] = leaf.astype(BF)
    for i in range(512 // NBLK):
        basis_copy(i, 0).wait()
        basis_copy(i, 1).wait()
    lax.fori_loop(0, 32, lambda i, _: far_rows(i, S, rounded, F), None, unroll=4)
    pot_ref[...] = F[...] + near_rows(N)


def call(table, coarse, src, vec, length, parent, octant, near, ext, m2l, l2l, basis):
    vmem = pl.BlockSpec(memory_space=pltpu.VMEM)
    hbm = pl.BlockSpec(memory_space=pl.ANY)
    return pl.pallas_call(
        kernel,
        out_shape=(jax.ShapeDtypeStruct((512, 256), F32), jax.ShapeDtypeStruct((128, 128), F32)),
        in_specs=[vmem] * 9 + [hbm] * 3,
        out_specs=(vmem, vmem),
        scratch_shapes=[
            pltpu.VMEM((10, 512, 16, 256), BF),
            pltpu.VMEM((2, 16 * NBLK, 128), F32),
            pltpu.VMEM((24, 512, 256), BF),
            pltpu.VMEM((24, 256, 256), BF),
            pltpu.VMEM((512, 256), BF),
            pltpu.VMEM((256, 128), F32),
            pltpu.VMEM((256, 128), F32),
            pltpu.VMEM((256, 128), F32),
            pltpu.VMEM((4, 2, 128, 128), F32),
            pltpu.VMEM((4, 5, 32, 128), F32),
            pltpu.VMEM((4, 3, 32, 128), F32),
            pltpu.VMEM((4, 32, 4, 8, 128), F32),
            pltpu.VMEM((4, 32, 128), F32),
            pltpu.VMEM((128, 128), F32),
            pltpu.SemaphoreType.DMA((2,)),
            pltpu.SemaphoreType.DMA((512 // NBLK, 2)),
        ],
        compiler_params=pltpu.CompilerParams(vmem_limit_bytes=63 << 20),
    )(table, coarse, src, vec, length, parent, octant, near, ext, m2l, l2l, basis.reshape(512, 2, 16, 256))


def shifted_2(shard, axis, by):
    peers = lax.axis_size(axis)
    pairs = [(i, i + by) for i in range(peers) if 0 <= i + by < peers]
    return lax.ppermute(shard, axis, pairs)


def shards(multipole, coarse_local, send_rows, list_src, list_vec, list_len, parent_of, octant, m2l_ops, l2l_ops, near_list, positions, charges, basis):
    ids = send_rows.reshape(-1)
    pick = (ids[:, None] == jnp.arange(512, dtype=I32)[None, :]).astype(BF)
    outgoing = dot(pick, multipole).astype(BF).reshape(128, 16, 256)
    incoming = lax.all_to_all(outgoing, ("gx", "gy"), split_axis=0, concat_axis=0, tiled=True)
    table = jnp.concatenate([multipole, incoming.reshape(-1, 256)], axis=0)
    whole = lax.all_gather(coarse_local, "gx", axis=0, tiled=True)
    data = jnp.concatenate([positions, charges[None, :]], axis=0).reshape(4, 128, 128)
    lower = shifted_2(data[:, 120:], ("gx", "gy"), 1)
    upper = shifted_2(data[:, :8], ("gx", "gy"), -1)
    ext = jnp.concatenate([lower, data, upper, jnp.zeros((4, 112, 128), F32)], axis=1)
    leaf, pot = call(
        table, whole, list_src, list_vec, list_len.reshape(4, 128), parent_of.reshape(4, 128), octant.reshape(4, 128),
        near_list, ext, m2l_ops, l2l_ops, basis,
    )
    return leaf, pot.reshape(-1)


def solution(mesh):
    both = ("gx", "gy")
    placed = (
        P(both, None), P("gx", None), P(both, None, None), P(both, None), P(both, None), P(both), P(both), P(both),
        P(), P(), P(both, None), P(None, both), P(both), P(both, None),
    )
    return jax.shard_map(shards, mesh=mesh, in_specs=placed, out_specs=(P(both, None), P(both)), check_vma=False)
```

```python
import functools

import jax
import jax.numpy as jnp
from jax import lax
from jax.experimental import pallas as pl
from jax.experimental.pallas import tpu as pltpu
from jax.sharding import PartitionSpec as P

BF = jnp.bfloat16
F8 = jnp.float8_e4m3fn
F32 = jnp.float32
I32 = jnp.int32
SOFT = 0.01


def iota(shape, axis):
    return lax.broadcasted_iota(I32, shape, axis)


def dot(a, b):
    return jnp.dot(a, b, preferred_element_type=F32)


def dot_nt(a, b):
    return lax.dot_general(a, b, (((1,), (1,)), ((), ())), preferred_element_type=F32)


def column(row):
    return jnp.broadcast_to(row, (128, 128)).T


def lanes(x, idx):
    return jnp.take_along_axis(x, idx, axis=1, mode="promise_in_bounds")


def onehot(rows, code):
    ids = iota((rows, 128), 0).astype(F32).astype(BF)
    return jnp.where(ids == jnp.broadcast_to(code, (rows, 128)).astype(BF), jnp.ones((), BF), jnp.zeros((), BF)).astype(F8)


def codes(src_ref, vec_ref, len_ref, hi0, hi1, lo):
    parts = []
    for b in range(4):
        cells = pl.ds(128 * b, 128)
        used = iota((64, 128), 0) < len_ref[pl.ds(b, 1), :]
        src = src_ref[:, cells]
        high = jnp.where(used, vec_ref[:, cells] + 16 * (src >> 8), -1).astype(F32)
        parts.append((high, (src & 255).astype(F32)))
    first = iota((128, 128), 1) < 64
    for b in range(2):
        rows = pl.ds(128 * b, 128)
        high = jnp.concatenate([parts[b][0], parts[b + 2][0]], 0).T
        hi0[rows, :] = jnp.where(first, high, -1.0)
        hi1[rows, :] = jnp.where(first, -1.0, high)
        lo[rows, :] = jnp.concatenate([parts[b][1], parts[b + 2][1]], 0).T


def count_pair(p, hi0, hi1, lo, S):
    a = jnp.concatenate([onehot(160, hi0[pl.ds(p, 1), :]), onehot(160, hi1[pl.ds(p, 1), :])], 0)
    s = dot_nt(a, onehot(256, lo[pl.ds(p, 1), :])).astype(BF)
    for t in range(10):
        S[t, p] = s[16 * t : 16 * t + 16]
        S[t, p + 256] = s[160 + 16 * t : 176 + 16 * t]


def near_prepare(E, near_ref, XT, Y, tgt, src):
    for f in range(4):
        for h in range(2):
            XT[f, h] = E[f, pl.ds(128 * h, 128), :].T
        own = E[f, pl.ds(8, 128), :].T if f < 3 else None
        lane = iota((32, 128), 1)
        for b in range(5):
            y = None
            for q in range(4):
                g = lanes(XT[f, b // 4, pl.ds(32 * q, 32), :], 32 * (b % 4) + (lane >> 2))
                y = g if q == 0 else jnp.where((lane & 3) == q, g, y)
            Y[f, b] = y
        if f < 3:
            for b in range(4):
                y = None
                for q in range(4):
                    g = lanes(own[32 * q : 32 * q + 32], 32 * b + (lane >> 2))
                    y = g if q == 0 else jnp.where((lane & 3) == q, g, y)
                tgt[b, f] = y
    for b in range(4):
        listed = near_ref[:, pl.ds(128 * b, 128)]
        for n in range(8):
            idx = jnp.broadcast_to(listed[n : n + 1] - 128 * b, (32, 128))
            inside, wrapped = idx < 128, idx & 127
            for f in range(4):
                g = jnp.where(inside, lanes(Y[f, b], wrapped), lanes(Y[f, b + 1], wrapped))
                for s in range(4):
                    src[b, 4 * n + s, f] = g[8 * s : 8 * s + 8]


def near_unit(b, jj, J, tgt, src, N):
    ts = [
        [jnp.broadcast_to(tgt[b, f, pl.ds(jj * J + j, 1), :], (8, 128)) for f in range(3)] for j in range(J)
    ]
    acc = [jnp.zeros((8, 128), F32) for _ in range(J)]
    for m in range(32):
        x, y, z, q = (src[b, m, f] for f in range(4))
        for j in range(J):
            dx, dy, dz = x - ts[j][0], y - ts[j][1], z - ts[j][2]
            acc[j] = acc[j] + q * lax.rsqrt(dx * dx + dy * dy + (dz * dz + SOFT))
    for j in range(J):
        N[b, pl.ds(jj * J + j, 1), :] = jnp.sum(acc[j], 0, keepdims=True)


def near_rows(N):
    lane = iota((32, 128), 1)
    parts = []
    for q in range(4):
        z = None
        for b in range(4):
            g = lanes(N[b], 4 * (lane & 31) + q)
            z = g if b == 0 else jnp.where((lane >> 5) == b, g, z)
        parts.append(z)
    return jnp.concatenate(parts, 0).T


def group(i, n, own, incoming, S, G, Gb):
    rows = 16 * n
    lhs = [S[t, pl.ds(i * n, n)].reshape(rows, 256) for t in range(10)]
    g = dot(jnp.concatenate(lhs[:2], 1), own[...]) + dot(jnp.concatenate(lhs[2:], 1), incoming[...].reshape(2048, 256))
    G[0] = g[:, :128]
    G[1] = g[:, 128:]
    for v in range(16):
        Gb[v, pl.ds(i * n, n), :] = jnp.concatenate(
            [G[0, pl.ds(v, n, stride=16), :], G[1, pl.ds(v, n, stride=16), :]], 1
        ).astype(BF)


def coarse_rows(parent_ref, octant_ref, coarse, Gb):
    for b in range(4):
        parent = column(parent_ref[pl.ds(b, 1), :].astype(F32))
        octant = column(octant_ref[pl.ds(b, 1), :].astype(F32))
        lane = iota((128, 128), 1).astype(F32)
        pick = jnp.concatenate([(parent == lane).astype(F32), (parent == lane + 128.0).astype(F32)], 1).astype(BF)
        rows = dot(pick, coarse[...].reshape(256, 256))
        octant = jnp.concatenate([octant, octant], 1)
        for o in range(8):
            Gb[16 + o, pl.ds(128 * b, 128), :] = jnp.where(octant == float(o), rows, 0.0).astype(BF)


def far_rows(i, S, rounded, F):
    pieces = []
    for c in range(16):
        pieces += [S[0, i * 16 + c], S[1, i * 16 + c]]
    r = dot_nt(rounded[pl.ds(pl.multiple_of(16 * i, 16), 16), :], jnp.concatenate(pieces, 0))
    r = jnp.where(iota((16, 512), 0) == (iota((16, 512), 1) >> 5), r, 0.0)
    r = jnp.sum(r, 0, keepdims=True)
    for h in range(4):
        F[pl.ds(4 * i + h, 1), :] = r[:, 128 * h : 128 * h + 128]


def fill_data(pos_ref, charge_ref, E):
    for r in range(128):
        for f in range(3):
            E[f, pl.ds(8 + r, 1), :] = pos_ref[pl.ds(f, 1), pl.ds(128 * r, 128)]
    E[3, pl.ds(8, 128), :] = charge_ref[...]


def pick_rows(send_ref, multipole, SG, outgoing):
    lane = iota((128, 128), 1).astype(F32)
    for jj in range(4):
        picks = []
        for j in range(4):
            ids = column(send_ref[pl.ds(4 * jj + j, 1), :].astype(F32))
            picks.append(jnp.concatenate([(ids == lane + 128.0 * h).astype(F32).astype(BF) for h in range(4)], 1))
        rows = dot(jnp.concatenate(picks, 0), multipole[...])
        SG[0, pl.ds(512 * jj, 512), :] = rows[:, :128]
        SG[1, pl.ds(512 * jj, 512), :] = rows[:, 128:]
    for d in range(128):
        rows = pl.ds(d, 16, stride=128)
        outgoing[d] = jnp.concatenate([SG[0, rows, :], SG[1, rows, :]], 1).astype(BF)


NBLK = 64
MESH = pl.DeviceIdType.MESH


def kernel(
    multipole_ref, coarse_ref, send_ref, src_ref, vec_ref, len_ref, parent_ref, octant_ref, near_ref, pos_ref, charge_ref,
    m2l_hbm, l2l_hbm, basis_hbm,
    leaf_ref, pot_ref,
    S, G, Gb, ops, rounded, hi0, hi1, lo, XT, Y, tgt, src, N, F, E, SG, outgoing, incoming, coarse,
    sem_ops, sem_basis, send_sem, recv_sem, coarse_send, coarse_recv, rim_send, rim_recv,
):
    gx, gy = lax.axis_index("gx"), lax.axis_index("gy")
    me = gx * 16 + gy
    E[:, pl.ds(0, 8), :] = jnp.zeros((4, 8, 128), F32)
    E[:, pl.ds(136, 120), :] = jnp.zeros((4, 120, 128), F32)

    barrier = pltpu.get_barrier_semaphore()

    def greet(o, _):
        d = lax.rem(me + o, 128)
        pl.semaphore_signal(barrier, inc=1, device_id=(d // 16, lax.rem(d, 16)), device_id_type=MESH)

    lax.fori_loop(1, 128, greet, None)
    ops_in = [
        pltpu.make_async_copy(m2l_hbm, ops.at[pl.ds(0, 16)], sem_ops.at[0]),
        pltpu.make_async_copy(l2l_hbm, ops.at[pl.ds(16, 8)], sem_ops.at[1]),
    ]
    for c in ops_in:
        c.start()
    fill_data(pos_ref, charge_ref, E)
    pick_rows(send_ref, multipole_ref, SG, outgoing)
    pl.semaphore_wait(barrier, 127)

    def send(o):
        d = lax.rem(me + o, 128)
        return pltpu.make_async_remote_copy(
            src_ref=outgoing.at[d], dst_ref=incoming.at[me], send_sem=send_sem, recv_sem=recv_sem,
            device_id=(d // 16, lax.rem(d, 16)), device_id_type=MESH,
        )

    def send_coarse(r):
        return pltpu.make_async_remote_copy(
            src_ref=coarse_ref, dst_ref=coarse.at[gx], send_sem=coarse_send, recv_sem=coarse_recv,
            device_id=(lax.rem(gx + r, 8), gy), device_id_type=MESH,
        )

    def send_rim(up):
        d = me + 1 if up else me - 1
        return pltpu.make_async_remote_copy(
            src_ref=E.at[:, pl.ds(128 if up else 8, 8)], dst_ref=E.at[:, pl.ds(0 if up else 136, 8)],
            send_sem=rim_send.at[int(up)], recv_sem=rim_recv.at[int(up)],
            device_id=(d // 16, lax.rem(d, 16)), device_id_type=MESH,
        )

    @pl.when(me < 127)
    def _():
        send_rim(True).start()

    @pl.when(me > 0)
    def _():
        send_rim(False).start()

    lax.fori_loop(1, 128, lambda o, _: send(o).start(), None)
    lax.fori_loop(1, 8, lambda r, _: send_coarse(r).start(), None)
    incoming[me] = outgoing[me]
    coarse[gx] = coarse_ref[...]

    codes(src_ref, vec_ref, len_ref, hi0, hi1, lo)
    lax.fori_loop(0, 256, lambda p, _: count_pair(p, hi0, hi1, lo, S), None, unroll=32)

    @pl.when(me > 0)
    def _():
        send_rim(True).wait_recv()
        send_rim(False).wait_send()

    @pl.when(me < 127)
    def _():
        send_rim(False).wait_recv()
        send_rim(True).wait_send()

    near_prepare(E, near_ref, XT, Y, tgt, src)
    for b in range(4):
        lax.fori_loop(0, 8, lambda jj, _: near_unit(b, jj, 4, tgt, src, N), None)

    def all_of(ref, n, send_sem, recv_sem):
        part = ref.at[pl.ds(0, n)]
        return pltpu.make_async_remote_copy(
            src_ref=part, dst_ref=part, send_sem=send_sem, recv_sem=recv_sem, device_id=(gx, gy), device_id_type=MESH
        )

    coarse_in = all_of(coarse, 7, coarse_send, coarse_recv)
    coarse_in.wait_send()
    coarse_in.wait_recv()
    coarse_rows(parent_ref, octant_ref, coarse, Gb)
    rows_in = all_of(incoming, 127, send_sem, recv_sem)
    rows_in.wait_send()
    rows_in.wait_recv()

    def basis_copy(i, h):
        cells = pl.ds(i * NBLK, NBLK)
        return pltpu.make_async_copy(basis_hbm.at[cells, h], S.at[h, cells], sem_basis.at[i, h])

    def block(i, _):
        group(i, NBLK, multipole_ref, incoming, S, G, Gb)
        basis_copy(i, 0).start()
        basis_copy(i, 1).start()

    lax.fori_loop(0, 512 // NBLK, block, None)
    for c in ops_in:
        c.wait()
    for h in range(2):
        rows = pl.ds(256 * h, 256)
        leaf = dot(jnp.concatenate([Gb[v, rows, :] for v in range(24)], 1), ops[...].reshape(24 * 256, 256))
        leaf_ref[rows, :] = leaf
        rounded[rows, :] = leaf.astype(BF)
    for i in range(512 // NBLK):
        basis_copy(i, 0).wait()
        basis_copy(i, 1).wait()
    lax.fori_loop(0, 32, lambda i, _: far_rows(i, S, rounded, F), None, unroll=4)
    pot_ref[...] = F[...] + near_rows(N)


def shards(
    multipole, coarse_local, send_rows, list_src, list_vec, list_len, parent_of, octant, m2l_ops, l2l_ops, near_list,
    positions, charges, basis,
):
    vmem = pl.BlockSpec(memory_space=pltpu.VMEM)
    hbm = pl.BlockSpec(memory_space=pl.ANY)
    dma = pltpu.SemaphoreType.DMA
    leaf, pot = pl.pallas_call(
        kernel,
        out_shape=(jax.ShapeDtypeStruct((512, 256), F32), jax.ShapeDtypeStruct((128, 128), F32)),
        in_specs=[vmem] * 11 + [hbm] * 3,
        out_specs=(vmem, vmem),
        scratch_shapes=[
            pltpu.VMEM((10, 512, 16, 256), BF),
            pltpu.VMEM((2, 16 * NBLK, 128), F32),
            pltpu.VMEM((24, 512, 256), BF),
            pltpu.VMEM((24, 256, 256), BF),
            pltpu.VMEM((512, 256), BF),
            pltpu.VMEM((256, 128), F32),
            pltpu.VMEM((256, 128), F32),
            pltpu.VMEM((256, 128), F32),
            pltpu.VMEM((4, 2, 128, 128), F32),
            pltpu.VMEM((4, 5, 32, 128), F32),
            pltpu.VMEM((4, 3, 32, 128), F32),
            pltpu.VMEM((4, 32, 4, 8, 128), F32),
            pltpu.VMEM((4, 32, 128), F32),
            pltpu.VMEM((128, 128), F32),
            pltpu.VMEM((4, 256, 128), F32),
            pltpu.VMEM((2, 2048, 128), F32),
            pltpu.VMEM((128, 16, 256), BF),
            pltpu.VMEM((128, 16, 256), BF),
            pltpu.VMEM((8, 32, 256), BF),
            dma((2,)), dma((512 // NBLK, 2)), dma, dma, dma, dma, dma((2,)), dma((2,)),
        ],
        compiler_params=pltpu.CompilerParams(vmem_limit_bytes=63 << 20, collective_id=0, has_side_effects=True),
    )(
        multipole, coarse_local, send_rows[0].T, list_src.T, list_vec.T, list_len.reshape(4, 128), parent_of.reshape(4, 128),
        octant.reshape(4, 128), near_list.T, positions, charges.reshape(128, 128), m2l_ops, l2l_ops,
        basis.reshape(512, 2, 16, 256),
    )
    return leaf, pot.reshape(-1)


def solution(mesh):
    both = ("gx", "gy")
    placed = (
        P(both, None), P("gx", None), P(both, None, None), P(both, None), P(both, None), P(both), P(both), P(both),
        P(), P(), P(both, None), P(None, both), P(both), P(both, None),
    )
    return jax.shard_map(shards, mesh=mesh, in_specs=placed, out_specs=(P(both, None), P(both)), check_vma=False)
```

```python
import functools

import jax
import jax.numpy as jnp
from jax import lax
from jax.experimental import pallas as pl
from jax.experimental.pallas import tpu as pltpu
from jax.sharding import PartitionSpec as P

BF = jnp.bfloat16
F8 = jnp.float8_e4m3fn
F32 = jnp.float32
I32 = jnp.int32
SOFT = 0.01


def iota(shape, axis):
    return lax.broadcasted_iota(I32, shape, axis)


def dot(a, b):
    return jnp.dot(a, b, preferred_element_type=F32)


def dot_nt(a, b):
    return lax.dot_general(a, b, (((1,), (1,)), ((), ())), preferred_element_type=F32)


def column(row):
    return jnp.broadcast_to(row, (128, 128)).T


def lanes(x, idx):
    return jnp.take_along_axis(x, idx, axis=1, mode="promise_in_bounds")


def onehot(rows, code):
    ids = iota((rows, 128), 0).astype(F32).astype(BF)
    return jnp.where(ids == jnp.broadcast_to(code, (rows, 128)).astype(BF), jnp.ones((), BF), jnp.zeros((), BF)).astype(F8)


def codes(src_ref, vec_ref, len_ref, hi0, hi1, lo):
    parts = []
    for b in range(4):
        cells = pl.ds(128 * b, 128)
        used = iota((64, 128), 0) < len_ref[pl.ds(b, 1), :]
        src = src_ref[:, cells]
        high = jnp.where(used, vec_ref[:, cells] + 16 * (src >> 8), -1).astype(F32)
        parts.append((high, (src & 255).astype(F32)))
    first = iota((128, 128), 1) < 64
    for b in range(2):
        rows = pl.ds(128 * b, 128)
        high = jnp.concatenate([parts[b][0], parts[b + 2][0]], 0).T
        hi0[rows, :] = jnp.where(first, high, -1.0)
        hi1[rows, :] = jnp.where(first, -1.0, high)
        lo[rows, :] = jnp.concatenate([parts[b][1], parts[b + 2][1]], 0).T


def count_pair(p, hi0, hi1, lo, S):
    a = jnp.concatenate([onehot(160, hi0[pl.ds(p, 1), :]), onehot(160, hi1[pl.ds(p, 1), :])], 0)
    s = dot_nt(a, onehot(256, lo[pl.ds(p, 1), :])).astype(BF)
    for t in range(10):
        S[t, p] = s[16 * t : 16 * t + 16]
        S[t, p + 256] = s[160 + 16 * t : 176 + 16 * t]


def near_prepare(E, near_ref, XT, Y, tgt, src):
    for f in range(4):
        for h in range(2):
            XT[f, h] = E[f, pl.ds(128 * h, 128), :].T
        own = E[f, pl.ds(8, 128), :].T if f < 3 else None
        lane = iota((32, 128), 1)
        for b in range(5):
            y = None
            for q in range(4):
                g = lanes(XT[f, b // 4, pl.ds(32 * q, 32), :], 32 * (b % 4) + (lane >> 2))
                y = g if q == 0 else jnp.where((lane & 3) == q, g, y)
            Y[f, b] = y
        if f < 3:
            for b in range(4):
                y = None
                for q in range(4):
                    g = lanes(own[32 * q : 32 * q + 32], 32 * b + (lane >> 2))
                    y = g if q == 0 else jnp.where((lane & 3) == q, g, y)
                tgt[b, f] = y
    for b in range(4):
        listed = near_ref[:, pl.ds(128 * b, 128)]
        for n in range(8):
            idx = jnp.broadcast_to(listed[n : n + 1] - 128 * b, (32, 128))
            inside, wrapped = idx < 128, idx & 127
            for f in range(4):
                g = jnp.where(inside, lanes(Y[f, b], wrapped), lanes(Y[f, b + 1], wrapped))
                for s in range(4):
                    src[b, 4 * n + s, f] = g[8 * s : 8 * s + 8]


def near_unit(b, jj, J, tgt, src, N):
    ts = [
        [jnp.broadcast_to(tgt[b, f, pl.ds(jj * J + j, 1), :], (8, 128)) for f in range(3)] for j in range(J)
    ]
    acc = [jnp.zeros((8, 128), F32) for _ in range(J)]
    for m in range(32):
        x, y, z, q = (src[b, m, f] for f in range(4))
        for j in range(J):
            dx, dy, dz = x - ts[j][0], y - ts[j][1], z - ts[j][2]
            acc[j] = acc[j] + q * lax.rsqrt(dx * dx + dy * dy + (dz * dz + SOFT))
    for j in range(J):
        N[b, pl.ds(jj * J + j, 1), :] = jnp.sum(acc[j], 0, keepdims=True)


def near_rows(N):
    lane = iota((32, 128), 1)
    parts = []
    for q in range(4):
        z = None
        for b in range(4):
            g = lanes(N[b], 4 * (lane & 31) + q)
            z = g if b == 0 else jnp.where((lane >> 5) == b, g, z)
        parts.append(z)
    return jnp.concatenate(parts, 0).T


def group(i, n, first, count, rows_of, S, G, add):
    rows = pl.ds(i * (16 * n), 16 * n)
    lhs = [S[first + t, pl.ds(i * n, n)].reshape(16 * n, 256) for t in range(count)]
    g = dot(jnp.concatenate(lhs, 1), rows_of)
    for h in range(2):
        part = g[:, 128 * h : 128 * h + 128]
        G[h, rows, :] = G[h, rows, :] + part if add else part


def coarse_rows(parent_ref, octant_ref, coarse, C, oct):
    for b in range(4):
        rows = pl.ds(128 * b, 128)
        parent = column(parent_ref[pl.ds(b, 1), :].astype(F32))
        oct[rows, :] = column(octant_ref[pl.ds(b, 1), :].astype(F32))
        lane = iota((128, 128), 1).astype(F32)
        pick = jnp.concatenate([(parent == lane).astype(F32), (parent == lane + 128.0).astype(F32)], 1).astype(BF)
        C[rows, :] = dot(pick, coarse[...].reshape(256, 256))


def leaves(h, n, G, C, oct, ops, leaf_ref, rounded):
    rows = pl.ds(h * n, n)
    parts = []
    for v in range(16):
        at = pl.ds(h * (16 * n) + v, n, stride=16)
        parts.append(jnp.concatenate([G[0, at, :], G[1, at, :]], 1).astype(BF))
    octant = jnp.concatenate([oct[rows, :]] * 2, 1)
    coarse = C[rows, :]
    for o in range(8):
        parts.append(jnp.where(octant == float(o), coarse, 0.0).astype(BF))
    leaf = dot(jnp.concatenate(parts, 1), ops[...].reshape(24 * 256, 256))
    leaf_ref[rows, :] = leaf
    rounded[rows, :] = leaf.astype(BF)


def far_rows(i, S, rounded, near, pot_ref):
    pieces = []
    for c in range(16):
        pieces += [S[0, i * 16 + c], S[1, i * 16 + c]]
    r = dot_nt(rounded[pl.ds(pl.multiple_of(16 * i, 16), 16), :], jnp.concatenate(pieces, 0))
    r = jnp.where(iota((16, 512), 0) == (iota((16, 512), 1) >> 5), r, 0.0)
    r = jnp.sum(r, 0, keepdims=True)
    for h in range(4):
        row = pl.ds(4 * i + h, 1)
        pot_ref[row, :] = near[row, :] + r[:, 128 * h : 128 * h + 128]


def fill_data(pos_ref, charge_ref, E):
    for r in range(128):
        for f in range(3):
            E[f, pl.ds(8 + r, 1), :] = pos_ref[pl.ds(f, 1), pl.ds(128 * r, 128)]
    E[3, pl.ds(8, 128), :] = charge_ref[...]


def pick_rows(send_ref, multipole, SG, outgoing):
    lane = iota((128, 128), 1).astype(F32)
    for jj in range(4):
        picks = []
        for j in range(4):
            ids = column(send_ref[pl.ds(4 * jj + j, 1), :].astype(F32))
            picks.append(jnp.concatenate([(ids == lane + 128.0 * h).astype(F32).astype(BF) for h in range(4)], 1))
        rows = dot(jnp.concatenate(picks, 0), multipole[...])
        SG[0, pl.ds(512 * jj, 512), :] = rows[:, :128]
        SG[1, pl.ds(512 * jj, 512), :] = rows[:, 128:]
    for d in range(128):
        rows = pl.ds(d, 16, stride=128)
        outgoing[d] = jnp.concatenate([SG[0, rows, :], SG[1, rows, :]], 1).astype(BF)


NBLK = 64
MESH = pl.DeviceIdType.MESH


def kernel(
    multipole_ref, coarse_ref, send_ref, src_ref, vec_ref, len_ref, parent_ref, octant_ref, near_ref, pos_ref, charge_ref,
    m2l_hbm, l2l_hbm, basis_hbm,
    leaf_ref, pot_ref,
    S, G, ops, rounded, C, oct, hi0, hi1, lo, XT, Y, tgt, src, N, nearpot, E, SG, outgoing, incoming, coarse,
    sem_ops, sem_basis, send_sem, recv_sem, coarse_send, coarse_recv, rim_send, rim_recv, entered,
):
    gx, gy = lax.axis_index("gx"), lax.axis_index("gy")
    me = gx * 16 + gy
    E[:, pl.ds(0, 8), :] = jnp.zeros((4, 8, 128), F32)
    E[:, pl.ds(136, 120), :] = jnp.zeros((4, 120, 128), F32)

    barrier = pltpu.get_barrier_semaphore()

    def greet(sem, dx, dy):
        pl.semaphore_signal(sem, inc=1, device_id=(lax.rem(gx + dx, 8), lax.rem(gy + dy, 16)), device_id_type=MESH)

    for r in range(1, 8):
        greet(barrier, r, 0)
    for r in range(1, 16):
        greet(barrier, 0, r)
    ops_in = [
        pltpu.make_async_copy(m2l_hbm, ops.at[pl.ds(0, 16)], sem_ops.at[0]),
        pltpu.make_async_copy(l2l_hbm, ops.at[pl.ds(16, 8)], sem_ops.at[1]),
    ]
    for c in ops_in:
        c.start()
    fill_data(pos_ref, charge_ref, E)
    pl.semaphore_wait(barrier, 22)
    for r in range(1, 8):
        greet(entered, r, 0)
    pick_rows(send_ref, multipole_ref, SG, outgoing)
    codes(src_ref, vec_ref, len_ref, hi0, hi1, lo)
    pl.semaphore_wait(entered, 7)

    def send(o):
        d = lax.rem(me + o, 128)
        return pltpu.make_async_remote_copy(
            src_ref=outgoing.at[d], dst_ref=incoming.at[me], send_sem=send_sem, recv_sem=recv_sem,
            device_id=(d // 16, lax.rem(d, 16)), device_id_type=MESH,
        )

    def send_coarse(r):
        return pltpu.make_async_remote_copy(
            src_ref=coarse_ref, dst_ref=coarse.at[gx], send_sem=coarse_send, recv_sem=coarse_recv,
            device_id=(lax.rem(gx + r, 8), gy), device_id_type=MESH,
        )

    def send_rim(up):
        d = me + 1 if up else me - 1
        return pltpu.make_async_remote_copy(
            src_ref=E.at[:, pl.ds(128 if up else 8, 8)], dst_ref=E.at[:, pl.ds(0 if up else 136, 8)],
            send_sem=rim_send.at[int(up)], recv_sem=rim_recv.at[int(up)],
            device_id=(d // 16, lax.rem(d, 16)), device_id_type=MESH,
        )

    @pl.when(me < 127)
    def _():
        send_rim(True).start()

    @pl.when(me > 0)
    def _():
        send_rim(False).start()

    for o in range(1, 4):
        send(o).start()
    incoming[me] = outgoing[me]
    coarse[gx] = coarse_ref[...]

    def count_and_send(i, _):
        for u in range(32):
            count_pair(i * 32 + u, hi0, hi1, lo, S)
            if u < 31:
                send(4 + i * 31 + u).start()

    lax.fori_loop(0, 4, count_and_send, None)
    lax.fori_loop(1, 8, lambda r, _: send_coarse(r).start(), None)

    @pl.when(me > 0)
    def _():
        send_rim(True).wait_recv()
        send_rim(False).wait_send()

    @pl.when(me < 127)
    def _():
        send_rim(False).wait_recv()
        send_rim(True).wait_send()

    near_prepare(E, near_ref, XT, Y, tgt, src)

    def count_and_near(i, _):
        for u in range(8):
            for w in range(4):
                count_pair(128 + i * 32 + 4 * u + w, hi0, hi1, lo, S)
            near_unit(i, u, 4, tgt, src, N)

    lax.fori_loop(0, 4, count_and_near, None)
    nearpot[...] = near_rows(N)
    blocks = 512 // NBLK
    lax.fori_loop(0, blocks, lambda i, _: group(i, NBLK, 0, 2, multipole_ref[...], S, G, False), None)

    def all_of(ref, n, send_sem, recv_sem):
        part = ref.at[pl.ds(0, n)]
        return pltpu.make_async_remote_copy(
            src_ref=part, dst_ref=part, send_sem=send_sem, recv_sem=recv_sem, device_id=(gx, gy), device_id_type=MESH
        )

    basis_in = [pltpu.make_async_copy(basis_hbm.at[:, h], S.at[h], sem_basis.at[h]) for h in range(2)]
    for c in basis_in:
        c.start()
    coarse_in = all_of(coarse, 7, coarse_send, coarse_recv)
    coarse_in.wait_send()
    coarse_in.wait_recv()
    coarse_rows(parent_ref, octant_ref, coarse, C, oct)
    rows_in = all_of(incoming, 127, send_sem, recv_sem)
    rows_in.wait_send()
    rows_in.wait_recv()
    lax.fori_loop(0, blocks, lambda i, _: group(i, NBLK, 2, 8, incoming[...].reshape(2048, 256), S, G, True), None)
    for c in ops_in:
        c.wait()
    for h in range(2):
        leaves(h, 256, G, C, oct, ops, leaf_ref, rounded)
    for c in basis_in:
        c.wait()
    lax.fori_loop(0, 32, lambda i, _: far_rows(i, S, rounded, nearpot, pot_ref), None, unroll=4)


def results(leaf_in, pot_in, leaf_out, pot_out):
    leaf_out[...] = leaf_in[...]
    pot_out[...] = pot_in[...]


def shards(
    multipole, coarse_local, send_rows, list_src, list_vec, list_len, parent_of, octant, m2l_ops, l2l_ops, near_list,
    positions, charges, basis,
):
    vmem = pl.BlockSpec(memory_space=pltpu.VMEM)
    hbm = pl.BlockSpec(memory_space=pl.ANY)
    dma = pltpu.SemaphoreType.DMA
    outs = (jax.ShapeDtypeStruct((512, 256), F32), jax.ShapeDtypeStruct((128, 128), F32))
    leaf, pot = pl.pallas_call(
        kernel,
        out_shape=outs,
        in_specs=[vmem] * 11 + [hbm] * 3,
        out_specs=(vmem, vmem),
        scratch_shapes=[
            pltpu.VMEM((10, 512, 16, 256), BF),
            pltpu.VMEM((2, 8192, 128), F32),
            pltpu.VMEM((24, 256, 256), BF),
            pltpu.VMEM((512, 256), BF),
            pltpu.VMEM((512, 256), F32),
            pltpu.VMEM((512, 128), F32),
            pltpu.VMEM((256, 128), F32),
            pltpu.VMEM((256, 128), F32),
            pltpu.VMEM((256, 128), F32),
            pltpu.VMEM((4, 2, 128, 128), F32),
            pltpu.VMEM((4, 5, 32, 128), F32),
            pltpu.VMEM((4, 3, 32, 128), F32),
            pltpu.VMEM((4, 32, 4, 8, 128), F32),
            pltpu.VMEM((4, 32, 128), F32),
            pltpu.VMEM((128, 128), F32),
            pltpu.VMEM((4, 256, 128), F32),
            pltpu.VMEM((2, 2048, 128), F32),
            pltpu.VMEM((128, 16, 256), BF),
            pltpu.VMEM((128, 16, 256), BF),
            pltpu.VMEM((8, 32, 256), BF),
            dma((2,)), dma((2,)), dma, dma, dma, dma, dma((2,)), dma((2,)), pltpu.SemaphoreType.REGULAR,
        ],
        compiler_params=pltpu.CompilerParams(vmem_limit_bytes=63 << 20, collective_id=0, has_side_effects=True),
    )(
        multipole, coarse_local, send_rows[0].T, list_src.T, list_vec.T, list_len.reshape(4, 128), parent_of.reshape(4, 128),
        octant.reshape(4, 128), near_list.T, positions, charges.reshape(128, 128), m2l_ops, l2l_ops,
        basis.reshape(512, 2, 16, 256),
    )
    leaf, pot = pl.pallas_call(
        results, out_shape=outs, in_specs=[vmem] * 2, out_specs=(vmem, vmem)
    )(leaf, pot)
    return leaf, pot.reshape(-1)


def solution(mesh):
    both = ("gx", "gy")
    placed = (
        P(both, None), P("gx", None), P(both, None, None), P(both, None), P(both, None), P(both), P(both), P(both),
        P(), P(), P(both, None), P(None, both), P(both), P(both, None),
    )
    return jax.shard_map(shards, mesh=mesh, in_specs=placed, out_specs=(P(both, None), P(both)), check_vma=False)
```
